32 devices in a mesh: pipe: 2 (over y), ctx: 4 (over x, core), dp: 4 (over z).
Axes of the slice: x: 2, y: 2, z: 4, core: 2. Of those that a mesh axis runs over, the one named last changes fastest.
Arguments:
- hidden_in: bfloat16 [2, 4, 2048, 3584], P('pipe', 'dp', 'ctx'), may hold values from -6 to 6
- selected: int32 [2, 4, 32, 16], P('pipe', 'dp', 'ctx'), may hold values from -1 to 31, as said below
- norm_gain: float32 [2, 3584], P('pipe'), may hold values from 0.1 to 1.9
- kv_weight: bfloat16 [2, 3584, 512], P('pipe', ('ctx', 'dp')), may hold values from -0.1875 to 0.1875
- gate_weight: bfloat16 [2, 28, 3584], P('pipe'), may hold values from -0.09375 to 0.09375
- saved_norm: bfloat16 [2, 4, 2048, 3584], P('pipe', 'dp', 'ctx'), may hold values from -6 to 6
- kv_cot: bfloat16 [2, 4, 2048, 512], P('pipe', 'dp', 'ctx'), may hold values from -0.15625 to 0.15625
- gate_cot: bfloat16 [2, 4, 2048, 28], P('pipe', 'dp', 'ctx'), may hold values from -0.15625 to 0.15625
Outputs:
- passed: bfloat16 [2, 4, 2048, 3584], P('pipe', 'dp', 'ctx')
- kv_grad: bfloat16 [2, 3584, 512], P('pipe', ('ctx', 'dp'))
- gate_grad: bfloat16 [2, 28, 3584], P('pipe', None, ('ctx', 'dp'))
The draws below stay inside these ranges and needn't reach their ends.
Inputs may be any that keep to these rules, and one draw needn't show every extreme that they name: `selected`: for query block b, entry 0 is b; then come min(b, 15) distinct blocks below b in random order, then -1 in the remaining entries.
All inputs are finite; a program needn't handle non-finite values.
Results may differ from the reference program's by a relative error of at most 0.0061.
Values may be sent and summed in bfloat16 or wider, within the bound.
A program may use at most 128 MiB of HBM per device.

```python
import math
import jax
import jax.numpy as jnp
from jax import lax

H = 28
HD = 128
KVH = 2
BLOCK = 64
SEL = 16
D = 3584
KVW = 512
SEQ_LEN = 2048
QBLOCKS = 32
SEQS = 4
SECTIONS = 2


def draw_selected(key, part):
    blocks_total = QBLOCKS
    spread = 1 << 20
    ranking = jax.random.randint(key, (SECTIONS, SEQS, blocks_total, blocks_total), 0, spread, dtype=jnp.int32)
    ranking = ranking * blocks_total + jnp.arange(blocks_total, dtype=jnp.int32)
    earlier = jnp.arange(blocks_total, dtype=jnp.int32)[None, :] < jnp.arange(blocks_total, dtype=jnp.int32)[:, None]
    ranked = jnp.where(earlier, ranking, spread * blocks_total + blocks_total)
    ordering = jnp.argsort(ranked, axis=-1, stable=True)[..., :SEL - 1].astype(jnp.int32)
    own_block = jnp.broadcast_to(jnp.arange(blocks_total, dtype=jnp.int32)[:, None], (SECTIONS, SEQS, blocks_total, 1))
    usable = ordering < own_block
    picked = jnp.where(usable, ordering, -1)
    return jnp.concatenate([own_block, picked], axis=-1).astype(jnp.int32)


def levels(own_key, extent, shards, smallest, high):
    def one(axis_at, shards_of):
        draws = jax.random.uniform(jax.random.fold_in(jax.random.fold_in(own_key, 6), axis_at), (shards_of,), jnp.float32, smallest / len(shards), high / len(shards))
        return jnp.repeat(jnp.exp(draws), extent[axis_at] // shards_of).reshape((-1,) + (1,) * (len(extent) - axis_at - 1))

    level = one(*shards[0])
    for cut in shards[1:]:
        level = level * one(*cut)
    return level


def normal_values(stream_key, shape, width, most, cuts=(), kind=jnp.bfloat16):
    loudness = levels(stream_key, shape, cuts, -0.22, 0.18) if cuts else 1.0
    result = jax.random.normal(stream_key, shape, jnp.float32) * width * loudness
    return jnp.minimum(jnp.maximum(result, -most), most).astype(kind)


def setup_inputs(seed: int = 0) -> dict:
    seeds = jax.random.split(jax.random.key(seed), 9)
    hidden_in = normal_values(seeds[0], (SECTIONS, SEQS, SEQ_LEN, D), 1.0, 6.0, ((0, 2), (1, 4), (2, 4)))
    selected = draw_selected(jax.random.fold_in(seeds[8], 71), 0)
    norm_gain = jnp.clip(1.0 + 0.18 * jax.random.normal(seeds[2], (SECTIONS, D), jnp.float32), 0.1, 1.9)
    kv_weight = normal_values(seeds[3], (SECTIONS, D, KVW), (D // 4) ** -0.5, 0.1875, ((0, 2), (1, 16)))
    gate_weight = normal_values(seeds[4], (SECTIONS, H, D), D ** -0.5, 0.09375, ((0, 2),))
    saved_norm = normal_values(seeds[5], (SECTIONS, SEQS, SEQ_LEN, D), 1.0, 6.0, ((0, 2), (1, 4), (2, 4)))
    kv_cot = normal_values(seeds[6], (SECTIONS, SEQS, SEQ_LEN, KVW), ((SEQS * SEQ_LEN) ** -0.5), 0.15625, ((0, 2), (1, 4), (2, 4)))
    gate_cot = normal_values(seeds[7], (SECTIONS, SEQS, SEQ_LEN, H), ((SEQS * SEQ_LEN) ** -0.5), 0.15625, ((0, 2), (1, 4), (2, 4)))
    return {"hidden_in": hidden_in, "selected": selected, "norm_gain": norm_gain, "kv_weight": kv_weight, "gate_weight": gate_weight, "saved_norm": saved_norm, "kv_cot": kv_cot, "gate_cot": gate_cot}


epsilon = 1e-06

def attend_block(packed, key_rows, value_rows):
    query_block, block_picks, block_place = packed
    group = H // KVH
    chosen = jnp.maximum(block_picks, 0)
    key_tiles = jnp.take(key_rows, chosen, axis=0).reshape(SEL * BLOCK, KVH, HD).astype(jnp.float32)
    value_tiles = jnp.take(value_rows, chosen, axis=0).reshape(SEL * BLOCK, KVH, HD).astype(jnp.float32)
    query_heads = query_block.reshape(BLOCK, KVH, group, HD).astype(jnp.float32)
    score_scale = 1.0 / math.sqrt(HD)
    scores = jnp.einsum('qgjd,kgd->gjqk', query_heads, key_tiles) * score_scale
    key_place = (chosen[:, None] * BLOCK + jnp.arange(BLOCK, dtype=jnp.int32)[None, :]).reshape(-1)
    present = jnp.broadcast_to((block_picks >= 0)[:, None], (SEL, BLOCK)).reshape(-1)
    query_place = block_place * BLOCK + jnp.arange(BLOCK, dtype=jnp.int32)
    allowed = present[None, :] & (key_place[None, :] <= query_place[:, None])
    scores = jnp.where(allowed, scores, -1e+30)
    row_max = lax.optimization_barrier(jnp.max(scores, axis=-1, keepdims=True))
    weights = jnp.exp(scores - row_max)
    denominator = lax.optimization_barrier(jnp.sum(weights, axis=-1))
    weights_low = lax.optimization_barrier(weights.astype(jnp.bfloat16)).astype(jnp.float32)
    blended = jnp.einsum('gjqk,kgd->qgjd', weights_low, value_tiles)
    blended = blended / jnp.transpose(denominator, (2, 0, 1))[..., None]
    return blended.reshape(BLOCK, H * HD)

def section_layer(current, picks, gain, kv_rows, gate_rows):
    hidden = current.astype(jnp.float32)
    length = hidden.shape[0]
    normed = (hidden * lax.rsqrt(lax.optimization_barrier(jnp.mean(hidden * hidden, axis=-1, keepdims=True)) + epsilon) * gain.astype(jnp.float32)).astype(jnp.bfloat16)
    normed = lax.optimization_barrier(normed)
    projected = jnp.dot(normed, kv_rows, preferred_element_type=jnp.float32).astype(jnp.bfloat16)
    projected = lax.optimization_barrier(projected)
    half_width = KVH * HD
    blocks_here = length // BLOCK
    key_rows = projected[:, :half_width].reshape(blocks_here, BLOCK, KVH, HD)
    value_rows = projected[:, half_width:].reshape(blocks_here, BLOCK, KVH, HD)
    gating = jax.nn.sigmoid(jnp.dot(normed, gate_rows.T, preferred_element_type=jnp.float32))
    places = jnp.arange(blocks_here, dtype=jnp.int32)
    attended = lax.map(lambda packed: attend_block(packed, key_rows, value_rows), (normed.reshape(blocks_here, BLOCK, H * HD), picks, places))
    attended = attended.reshape(length, H, HD)
    section_out = hidden.reshape(length, H, HD) + gating[:, :, None] * attended
    return section_out.reshape(length, H * HD).astype(jnp.bfloat16)

def reference(hidden_in, selected, norm_gain, kv_weight, gate_weight, saved_norm, kv_cot, gate_cot):
    outputs = []
    kv_sums = []
    gate_sums = []
    for section in range(SECTIONS):

        def one_sequence(packed):
            return section_layer(packed[0], packed[1], norm_gain[section], kv_weight[section], gate_weight[section])
        outputs.append(lax.map(one_sequence, (hidden_in[section], selected[section])))
        flat_saved = saved_norm[section].reshape(-1, H * HD)
        flat_kv = kv_cot[section].reshape(-1, 2 * KVH * HD)
        flat_gate = gate_cot[section].reshape(-1, H)
        kv_sums.append(jnp.dot(flat_saved.T, flat_kv, preferred_element_type=jnp.float32).astype(jnp.bfloat16))
        gate_sums.append(jnp.dot(flat_gate.T, flat_saved, preferred_element_type=jnp.float32).astype(jnp.bfloat16))
    passed = jnp.roll(jnp.stack(outputs), 1, axis=0)
    return (passed, jnp.stack(kv_sums), jnp.stack(gate_sums))
```

```python
import functools
import math

import jax
import jax.numpy as jnp
from jax import lax
from jax.experimental import pallas as pl
from jax.experimental.pallas import tpu as pltpu
from jax.sharding import PartitionSpec as P

HD = 128
KVH = 2
BLOCK = 64
CHUNKS = 4

epsilon = 1e-06


def passed_along(block, axis, distance):
    devices = range(lax.axis_size(axis))
    route = [((i - distance) % len(devices), i) for i in devices]
    return lax.ppermute(block, axis, route)


def norm_kernel(hidden_ref, gain_ref, gate_ref, normed_ref, gating_ref):
    hidden = hidden_ref[...].astype(jnp.float32)
    scale = lax.rsqrt(jnp.mean(hidden * hidden, axis=-1, keepdims=True) + epsilon)
    normed = (hidden * scale * gain_ref[...]).astype(jnp.bfloat16)
    normed_ref[...] = normed
    logits = lax.dot_general(
        normed, gate_ref[...], (((1,), (1,)), ((), ())), preferred_element_type=jnp.float32
    )
    gating_ref[...] = jax.nn.sigmoid(logits)


def norm_and_gate(hidden, gain, gate_rows):
    length, width = hidden.shape
    heads = gate_rows.shape[0]
    tile = 128
    return pl.pallas_call(
        norm_kernel,
        grid=(length // tile,),
        in_specs=[
            pl.BlockSpec((tile, width), lambda i: (i, 0)),
            pl.BlockSpec((1, width), lambda i: (0, 0)),
            pl.BlockSpec((heads, width), lambda i: (0, 0)),
        ],
        out_specs=[
            pl.BlockSpec((tile, width), lambda i: (i, 0)),
            pl.BlockSpec((tile, heads), lambda i: (i, 0)),
        ],
        out_shape=[
            jax.ShapeDtypeStruct((length, width), jnp.bfloat16),
            jax.ShapeDtypeStruct((length, heads), jnp.float32),
        ],
        cost_estimate=pl.CostEstimate(
            flops=2 * length * width * 128, bytes_accessed=8 * length * width, transcendentals=0
        ),
    )(hidden, gain, gate_rows)


def grads_kernel(per_tile, rows, heads, saved_ref, kv_ref, gate_ref, out_ref):
    saved = saved_ref[...]
    kv = lax.dot_general(
        saved, kv_ref[...], (((0,), (0,)), ((), ())), preferred_element_type=jnp.float32
    )
    gate = lax.dot_general(
        gate_ref[...], saved, (((0,), (0,)), ((), ())), preferred_element_type=jnp.float32
    )
    out_ref[:, :rows, :] = kv.reshape(per_tile, rows, kv.shape[-1]).astype(out_ref.dtype)
    out_ref[:, rows:, :] = jnp.zeros_like(out_ref[:, rows:, :])
    for k in range(per_tile):
        out_ref[k, rows : rows + heads, :rows] = gate[:, k * rows : (k + 1) * rows].astype(
            out_ref.dtype
        )


def local_grads(saved, kv_cot, gate_cot, shards):
    length, width = saved.shape
    kv_width = kv_cot.shape[1]
    heads = gate_cot.shape[1]
    padded = -(-heads // 8) * 8
    tile = width // 4
    rows = width // shards
    per_tile = tile // rows
    return pl.pallas_call(
        functools.partial(grads_kernel, per_tile, rows, heads),
        grid=(width // tile,),
        in_specs=[
            pl.BlockSpec((length, tile), lambda i: (0, i)),
            pl.BlockSpec((length, kv_width), lambda i: (0, 0)),
            pl.BlockSpec((length, heads), lambda i: (0, 0)),
        ],
        out_specs=pl.BlockSpec((per_tile, rows + padded, kv_width), lambda i: (i, 0, 0)),
        out_shape=jax.ShapeDtypeStruct((shards, rows + padded, kv_width), jnp.float32),
        cost_estimate=pl.CostEstimate(
            flops=2 * length * width * kv_width,
            bytes_accessed=2 * length * width + 4 * width * kv_width,
            transcendentals=0,
        ),
    )(saved, kv_cot, gate_cot)


def attend_kernel(
    first, entries, picks_ref, place_ref, normed_ref, hidden_ref, gating_ref, kv_ref, out_ref,
    picked_ref, values_ref,
):
    step = first + pl.program_id(0)
    place = place_ref[0] + step
    keys = entries * BLOCK
    heads = gating_ref.shape[-1]
    group = heads // KVH
    half = group // 2
    scale = math.log2(math.e) / math.sqrt(HD)
    for c in range(entries):
        chosen = jnp.maximum(picks_ref[step, c], 0)
        tile = kv_ref[pl.ds(pl.multiple_of(chosen * BLOCK, BLOCK), BLOCK), :]
        span = slice(c * BLOCK, (c + 1) * BLOCK)
        for g in range(KVH):
            picked_ref[g, span, :] = tile[:, g * HD : (g + 1) * HD]
            values_ref[g, span, :HD] = tile[:, (KVH + g) * HD : (KVH + g + 1) * HD]
            values_ref[g, span, HD:] = jnp.ones((BLOCK, HD), jnp.bfloat16)
    column = lax.broadcasted_iota(jnp.int32, (BLOCK, keys), 1)
    row = lax.broadcasted_iota(jnp.int32, (BLOCK, keys), 0)
    last = jnp.where(column < BLOCK, row, (place + 1) * BLOCK - 1)
    bias = jnp.where(column <= last, 0.0, -1e30).astype(jnp.float32)
    gating = gating_ref[...]
    for g in range(KVH):
        k_all = picked_ref[g]
        v_all = values_ref[g]
        for part in range(0, group, half):
            first_head = g * group + part
            query = jnp.concatenate(
                [
                    normed_ref[:, (first_head + j) * HD : (first_head + j + 1) * HD]
                    for j in range(half)
                ],
                axis=0,
            )
            scores = lax.dot_general(
                query, k_all, (((1,), (1,)), ((), ())), preferred_element_type=jnp.float32
            )
            scores = (scores.reshape(half, BLOCK, keys) * scale + bias[None]).reshape(
                half * BLOCK, keys
            )
            top = jnp.max(scores, axis=-1, keepdims=True)
            weights = jnp.exp2(scores - top).astype(jnp.bfloat16)
            blended = jnp.dot(weights, v_all, preferred_element_type=jnp.float32)
            attended = blended[:, :HD] / blended[:, HD:]
            for j in range(half):
                h = first_head + j
                span = slice(h * HD, (h + 1) * HD)
                base = hidden_ref[:, span].astype(jnp.float32)
                piece = attended[j * BLOCK : (j + 1) * BLOCK]
                out_ref[:, span] = (base + gating[:, h : h + 1] * piece).astype(jnp.bfloat16)


def attend(first, count, picks, place, normed, hidden, gating, sequence_kv):
    width = normed.shape[1]
    heads = gating.shape[1]
    total, kv_width = sequence_kv.shape
    entries = picks.shape[1]
    return pl.pallas_call(
        functools.partial(attend_kernel, first, entries),
        grid_spec=pltpu.PrefetchScalarGridSpec(
            num_scalar_prefetch=2,
            grid=(count,),
            in_specs=[
                pl.BlockSpec((BLOCK, width), lambda i, *_: (first + i, 0)),
                pl.BlockSpec((BLOCK, width), lambda i, *_: (first + i, 0)),
                pl.BlockSpec((BLOCK, heads), lambda i, *_: (first + i, 0)),
                pl.BlockSpec((total, kv_width), lambda i, *_: (0, 0)),
            ],
            out_specs=pl.BlockSpec((BLOCK, width), lambda i, *_: (i, 0)),
            scratch_shapes=[
                pltpu.VMEM((KVH, entries * BLOCK, HD), jnp.bfloat16),
                pltpu.VMEM((KVH, entries * BLOCK, 2 * HD), jnp.bfloat16),
            ],
        ),
        out_shape=jax.ShapeDtypeStruct((count * BLOCK, width), jnp.bfloat16),
        cost_estimate=pl.CostEstimate(
            flops=6 * count * BLOCK * width * entries * BLOCK,
            bytes_accessed=6 * count * BLOCK * width + 2 * total * kv_width,
            transcendentals=count * BLOCK * heads * entries * BLOCK,
        ),
    )(picks, place, normed, hidden, gating, sequence_kv)


def per_device(
    hidden_in, selected, norm_gain, kv_weight, gate_weight, saved_norm, kv_cot, gate_cot
):
    current = hidden_in[0, 0]
    picks = selected[0, 0]
    length = current.shape[0]
    shards = lax.axis_size("ctx") * lax.axis_size("dp")
    all_rows = lax.all_gather(kv_weight[0], ("ctx", "dp"), axis=0, tiled=True)
    normed, gating = norm_and_gate(current, norm_gain, gate_weight[0])
    grads = local_grads(saved_norm[0, 0], kv_cot[0, 0], gate_cot[0, 0], shards)
    projected = jnp.dot(normed, all_rows, preferred_element_type=jnp.float32).astype(jnp.bfloat16)
    sequence_kv = lax.all_gather(projected, "ctx", axis=0, tiled=True)
    grads, sequence_kv = lax.optimization_barrier((grads, sequence_kv))
    summed = lax.psum_scatter(grads, ("ctx", "dp"), scatter_dimension=0, tiled=True)[0]
    blocks_here = length // BLOCK
    place = (lax.axis_index("ctx") * blocks_here).astype(jnp.int32)[None]
    chunks = math.gcd(CHUNKS, blocks_here)
    count = blocks_here // chunks
    pieces = []
    for i in range(chunks):
        piece = attend(i * count, count, picks, place, normed, current, gating, sequence_kv)
        pieces.append(passed_along(piece, "pipe", 1))
    passed = jnp.concatenate(pieces, axis=0)[None, None]
    rows = kv_weight.shape[1]
    heads = gate_weight.shape[1]
    kv_grad = summed[None, :rows].astype(jnp.bfloat16)
    gate_grad = summed[None, rows : rows + heads, :rows].astype(jnp.bfloat16)
    return (passed, kv_grad, gate_grad)


def solution(mesh):
    in_specs = (
        P("pipe", "dp", "ctx", None),
        P("pipe", "dp", "ctx", None),
        P("pipe", None),
        P("pipe", ("ctx", "dp"), None),
        P("pipe", None, None),
        P("pipe", "dp", "ctx", None),
        P("pipe", "dp", "ctx", None),
        P("pipe", "dp", "ctx", None),
    )
    out_specs = (
        P("pipe", "dp", "ctx", None),
        P("pipe", ("ctx", "dp"), None),
        P("pipe", None, ("ctx", "dp")),
    )
    return jax.shard_map(
        per_device, mesh=mesh, in_specs=in_specs, out_specs=out_specs, check_vma=False
    )
```

```python
import functools
import math

import jax
import jax.numpy as jnp
from jax import lax
from jax.experimental import pallas as pl
from jax.experimental.pallas import tpu as pltpu
from jax.sharding import PartitionSpec as P


HD = 128
KVH = 2
BLOCK = 64
CHUNKS = 4

epsilon = 1e-06


def passed_along(block, axis, distance):
    devices = range(lax.axis_size(axis))
    route = [((i - distance) % len(devices), i) for i in devices]
    return lax.ppermute(block, axis, route)


def front_kernel(
    ranks, levels, hidden_hbm, gain_ref, gate_ref, weight_ref, saved_hbm, kv_cot_ref, gate_cot_ref,
    normed_hbm, gating_ref, kv_hbm, grads_hbm,
    hidden_ref, normed_ref, saved_ref, full_ref, total_ref, kv_ref, grads_ref,
    load_sem, store_sem, send_sem, recv_sem, kv_send_sem, kv_recv_sem,
):
    pipe = lax.axis_index("pipe")
    mine = lax.axis_index("ctx")
    level = lax.axis_index("dp")
    across = lax.rem(mine + ranks // 2, ranks)
    beside = mine + 1 - 2 * lax.rem(mine, 2)
    corner = lax.rem(beside + ranks // 2, ranks)
    rows = weight_ref.shape[0]
    depth = levels * rows
    length, width = hidden_ref.shape
    tiles = kv_ref.shape[1]
    tile = length // tiles
    heads = gate_ref.shape[0]

    def at(rank, other):
        return (pipe, rank, other)

    loads = [
        pltpu.make_async_copy(hidden_hbm, hidden_ref, load_sem.at[0]),
        pltpu.make_async_copy(saved_hbm, saved_ref, load_sem.at[1]),
        pltpu.make_async_copy(weight_ref, full_ref.at[mine, level], load_sem.at[2]),
    ]
    for load in loads:
        load.start()

    partners = [at(mine, lax.rem(level + d, levels)) for d in range(1, levels)]
    partners += [at(across, level), at(beside, level)]
    barrier = pltpu.get_barrier_semaphore()
    for partner in partners:
        pl.semaphore_signal(
            barrier, inc=1, device_id=partner, device_id_type=pl.DeviceIdType.MESH
        )
    pl.semaphore_wait(barrier, len(partners))

    sent = []

    def send(source, rank, other, target):
        copy = pltpu.make_async_remote_copy(
            src_ref=source,
            dst_ref=full_ref.at[rank, other],
            send_sem=send_sem.at[len(sent)],
            recv_sem=recv_sem.at[rank, other],
            device_id=target,
            device_id_type=pl.DeviceIdType.MESH,
        )
        copy.start()
        sent.append(copy)

    def arrived(rank, other):
        pltpu.make_async_remote_copy(
            src_ref=full_ref.at[rank, other],
            dst_ref=full_ref.at[rank, other],
            send_sem=send_sem.at[0],
            recv_sem=recv_sem.at[rank, other],
            device_id=at(beside, level),
            device_id_type=pl.DeviceIdType.MESH,
        ).wait_recv()

    send(weight_ref, mine, level, at(across, level))
    for d in range(1, levels):
        send(weight_ref, mine, level, at(mine, lax.rem(level + d, levels)))
    send(weight_ref, mine, level, at(beside, level))

    loads[0].wait()

    def norm_tile(i, carry):
        span = pl.ds(pl.multiple_of(i * 64, 64), 64)
        hidden = hidden_ref[span, :].astype(jnp.float32)
        scale = lax.rsqrt(jnp.mean(hidden * hidden, axis=-1, keepdims=True) + epsilon)
        normed_ref[span, :] = (hidden * scale * gain_ref[...]).astype(jnp.bfloat16)
        return carry

    lax.fori_loop(0, length // 64, norm_tile, 0)
    stores = []

    def store(source, target):
        copy = pltpu.make_async_copy(source, target, store_sem.at[len(stores)])
        copy.start()
        stores.append(copy)

    parts = grads_ref.shape[0]
    per_part = grads_ref.shape[1]
    columns = width // parts

    def grad_part(i):
        saved = saved_ref[:, i * columns : (i + 1) * columns]
        kv = lax.dot_general(
            saved, kv_cot_ref[...], (((0,), (0,)), ((), ())), preferred_element_type=jnp.float32
        )
        gate = lax.dot_general(
            gate_cot_ref[...], saved, (((0,), (0,)), ((), ())), preferred_element_type=jnp.float32
        )
        grads_ref[i, :, :rows, :] = kv.reshape(per_part, rows, kv.shape[-1])
        grads_ref[i, :, rows:, :] = jnp.zeros_like(grads_ref[i, :, rows:, :])
        for k in range(per_part):
            grads_ref[i, k, rows : rows + heads, :rows] = gate[:, k * rows : (k + 1) * rows]

    loads[1].wait()
    loads[2].wait()
    for d in range(max(levels, parts)):
        if d < levels - 1:
            other = lax.rem(level + levels - 1 - d, levels)
            arrived(mine, other)
            send(full_ref.at[mine, other], mine, other, at(across, level))
            send(full_ref.at[mine, other], mine, other, at(beside, level))
        if d < levels:
            other = lax.rem(level + levels - d, levels)
            arrived(across, other)
            send(full_ref.at[across, other], across, other, at(beside, level))
        if d < parts:
            grad_part(d)
            if d > 0:
                store(grads_ref.at[d - 1], grads_hbm.at[d - 1])
    store(normed_ref, normed_hbm)

    def term(rank, first, count):
        span = pl.ds(pl.multiple_of(rank * depth, 128), depth)
        return jnp.dot(
            normed_ref[first : first + count, span],
            full_ref[rank].reshape(depth, full_ref.shape[-1]),
            preferred_element_type=jnp.float32,
        )

    total_ref[...] = term(mine, 0, length)
    store(grads_ref.at[parts - 1], grads_hbm.at[parts - 1])
    total_ref[...] += term(across, 0, length)
    for d in range(levels):
        arrived(beside, lax.rem(level + levels - d, levels))
    total_ref[...] += term(beside, 0, length)
    for d in range(levels):
        arrived(corner, lax.rem(level + levels - d, levels))

    kv_sent = []

    def kv_send(rank, t, target):
        copy = pltpu.make_async_remote_copy(
            src_ref=kv_ref.at[rank, t],
            dst_ref=kv_ref.at[rank, t],
            send_sem=kv_send_sem.at[len(kv_sent)],
            recv_sem=kv_recv_sem.at[rank, t],
            device_id=target,
            device_id_type=pl.DeviceIdType.MESH,
        )
        copy.start()
        kv_sent.append(copy)

    def kv_arrived(rank, t):
        pltpu.make_async_remote_copy(
            src_ref=kv_ref.at[rank, t],
            dst_ref=kv_ref.at[rank, t],
            send_sem=kv_send_sem.at[0],
            recv_sem=kv_recv_sem.at[rank, t],
            device_id=at(beside, level),
            device_id_type=pl.DeviceIdType.MESH,
        ).wait_recv()

    def publish(t):
        kv_send(mine, t, at(across, level))
        kv_send(mine, t, at(beside, level))

    for t in range(tiles):
        span = slice(t * tile, (t + 1) * tile)
        projected = total_ref[span, :] + term(corner, t * tile, tile)
        kv_ref[mine, t] = projected.astype(jnp.bfloat16)
        if t > 0:
            publish(t - 1)
    logits = lax.dot_general(
        normed_ref[...], gate_ref[...], (((1,), (1,)), ((), ())),
        preferred_element_type=jnp.float32,
    )
    publish(tiles - 1)
    gating_ref[...] = jax.nn.sigmoid(logits)
    for t in range(tiles):
        kv_arrived(across, t)
        kv_send(across, t, at(beside, level))
    for t in range(tiles):
        kv_arrived(beside, t)
        kv_arrived(corner, t)
    store(kv_ref, kv_hbm)
    for copy in sent + kv_sent:
        copy.wait_send()
    for copy in stores:
        copy.wait()


def front(hidden, gain, gate_rows, weight, saved, kv_cot, gate_cot):
    ranks = lax.axis_size("ctx")
    levels = lax.axis_size("dp")
    length, width = hidden.shape
    heads = gate_rows.shape[0]
    rows, kv_width = weight.shape
    shards = ranks * levels
    parts = ranks
    tiles = 4
    padded = -(-heads // 8) * 8
    low, full = jnp.bfloat16, jnp.float32
    grads_shape = (parts, shards // parts, rows + padded, kv_width)
    kv_shape = (ranks, tiles, length // tiles, kv_width)
    vmem = pl.BlockSpec(memory_space=pltpu.VMEM)
    hbm = pl.BlockSpec(memory_space=pl.ANY)
    normed, gating, kv, grads = pl.pallas_call(
        functools.partial(front_kernel, ranks, levels),
        in_specs=[hbm, vmem, vmem, vmem, hbm, vmem, vmem],
        out_specs=[hbm, vmem, hbm, hbm],
        out_shape=[
            jax.ShapeDtypeStruct((length, width), low),
            jax.ShapeDtypeStruct((length, heads), full),
            jax.ShapeDtypeStruct(kv_shape, low),
            jax.ShapeDtypeStruct(grads_shape, full),
        ],
        scratch_shapes=[
            pltpu.VMEM((length, width), low),
            pltpu.VMEM((length, width), low),
            pltpu.VMEM((length, width), low),
            pltpu.VMEM((ranks, levels, rows, kv_width), low),
            pltpu.VMEM((length, kv_width), full),
            pltpu.VMEM(kv_shape, low),
            pltpu.VMEM(grads_shape, full),
            pltpu.SemaphoreType.DMA((3,)),
            pltpu.SemaphoreType.DMA((parts + 2,)),
            pltpu.SemaphoreType.DMA((4 * levels - 1,)),
            pltpu.SemaphoreType.DMA((ranks, levels)),
            pltpu.SemaphoreType.DMA((3 * tiles,)),
            pltpu.SemaphoreType.DMA((ranks, tiles)),
        ],
        compiler_params=pltpu.CompilerParams(
            collective_id=0, has_side_effects=True, vmem_limit_bytes=48 * 2**20
        ),
    )(hidden, gain, gate_rows, weight, saved, kv_cot, gate_cot)
    return (
        normed,
        gating,
        kv.reshape(ranks * length, kv_width),
        grads.reshape(shards, rows + padded, kv_width),
    )


def attend_kernel(
    first, entries, picks_ref, place_ref, normed_ref, hidden_ref, gating_ref, kv_ref, out_ref,
    picked_ref, values_ref,
):
    step = first + pl.program_id(0)
    place = place_ref[0] + step
    keys = entries * BLOCK
    heads = gating_ref.shape[-1]
    group = heads // KVH
    half = group // 2
    scale = math.log2(math.e) / math.sqrt(HD)
    for c in range(entries):
        chosen = jnp.maximum(picks_ref[step, c], 0)
        tile = kv_ref[pl.ds(pl.multiple_of(chosen * BLOCK, BLOCK), BLOCK), :]
        span = slice(c * BLOCK, (c + 1) * BLOCK)
        for g in range(KVH):
            picked_ref[g, span, :] = tile[:, g * HD : (g + 1) * HD]
            values_ref[g, span, :HD] = tile[:, (KVH + g) * HD : (KVH + g + 1) * HD]
            values_ref[g, span, HD:] = jnp.ones((BLOCK, HD), jnp.bfloat16)
    column = lax.broadcasted_iota(jnp.int32, (BLOCK, keys), 1)
    row = lax.broadcasted_iota(jnp.int32, (BLOCK, keys), 0)
    last = jnp.where(column < BLOCK, row, (place + 1) * BLOCK - 1)
    bias = jnp.where(column <= last, 0.0, -1e30).astype(jnp.float32)
    gating = gating_ref[...]
    for g in range(KVH):
        k_all = picked_ref[g]
        v_all = values_ref[g]
        for part in range(0, group, half):
            first_head = g * group + part
            query = jnp.concatenate(
                [
                    normed_ref[:, (first_head + j) * HD : (first_head + j + 1) * HD]
                    for j in range(half)
                ],
                axis=0,
            )
            scores = lax.dot_general(
                query, k_all, (((1,), (1,)), ((), ())), preferred_element_type=jnp.float32
            )
            scores = (scores.reshape(half, BLOCK, keys) * scale + bias[None]).reshape(
                half * BLOCK, keys
            )
            top = jnp.max(scores, axis=-1, keepdims=True)
            weights = jnp.exp2(scores - top).astype(jnp.bfloat16)
            blended = jnp.dot(weights, v_all, preferred_element_type=jnp.float32)
            attended = blended[:, :HD] / blended[:, HD:]
            for j in range(half):
                h = first_head + j
                span = slice(h * HD, (h + 1) * HD)
                base = hidden_ref[:, span].astype(jnp.float32)
                piece = attended[j * BLOCK : (j + 1) * BLOCK]
                out_ref[:, span] = (base + gating[:, h : h + 1] * piece).astype(jnp.bfloat16)


def attend(first, count, picks, place, normed, hidden, gating, sequence_kv):
    width = normed.shape[1]
    heads = gating.shape[1]
    total, kv_width = sequence_kv.shape
    entries = picks.shape[1]
    return pl.pallas_call(
        functools.partial(attend_kernel, first, entries),
        grid_spec=pltpu.PrefetchScalarGridSpec(
            num_scalar_prefetch=2,
            grid=(count,),
            in_specs=[
                pl.BlockSpec((BLOCK, width), lambda i, *_: (first + i, 0)),
                pl.BlockSpec((BLOCK, width), lambda i, *_: (first + i, 0)),
                pl.BlockSpec((BLOCK, heads), lambda i, *_: (first + i, 0)),
                pl.BlockSpec((total, kv_width), lambda i, *_: (0, 0)),
            ],
            out_specs=pl.BlockSpec((BLOCK, width), lambda i, *_: (i, 0)),
            scratch_shapes=[
                pltpu.VMEM((KVH, entries * BLOCK, HD), jnp.bfloat16),
                pltpu.VMEM((KVH, entries * BLOCK, 2 * HD), jnp.bfloat16),
            ],
        ),
        out_shape=jax.ShapeDtypeStruct((count * BLOCK, width), jnp.bfloat16),
        cost_estimate=pl.CostEstimate(
            flops=6 * count * BLOCK * width * entries * BLOCK,
            bytes_accessed=6 * count * BLOCK * width + 2 * total * kv_width,
            transcendentals=count * BLOCK * heads * entries * BLOCK,
        ),
    )(picks, place, normed, hidden, gating, sequence_kv)


def per_device(
    hidden_in, selected, norm_gain, kv_weight, gate_weight, saved_norm, kv_cot, gate_cot
):
    current = hidden_in[0, 0]
    picks = selected[0, 0]
    length = current.shape[0]
    normed, gating, sequence_kv, grads = front(
        current, norm_gain, gate_weight[0], kv_weight[0], saved_norm[0, 0], kv_cot[0, 0],
        gate_cot[0, 0],
    )
    summed = lax.psum_scatter(grads, ("ctx", "dp"), scatter_dimension=0, tiled=True)[0]
    blocks_here = length // BLOCK
    place = (lax.axis_index("ctx") * blocks_here).astype(jnp.int32)[None]
    chunks = math.gcd(CHUNKS, blocks_here)
    count = blocks_here // chunks
    pieces = []
    for i in range(chunks):
        piece = attend(i * count, count, picks, place, normed, current, gating, sequence_kv)
        pieces.append(passed_along(piece, "pipe", 1))
    passed = jnp.concatenate(pieces, axis=0)[None, None]
    rows = kv_weight.shape[1]
    heads = gate_weight.shape[1]
    kv_grad = summed[None, :rows].astype(jnp.bfloat16)
    gate_grad = summed[None, rows : rows + heads, :rows].astype(jnp.bfloat16)
    return (passed, kv_grad, gate_grad)


def solution(mesh):
    in_specs = (
        P("pipe", "dp", "ctx", None),
        P("pipe", "dp", "ctx", None),
        P("pipe", None),
        P("pipe", ("ctx", "dp"), None),
        P("pipe", None, None),
        P("pipe", "dp", "ctx", None),
        P("pipe", "dp", "ctx", None),
        P("pipe", "dp", "ctx", None),
    )
    out_specs = (
        P("pipe", "dp", "ctx", None),
        P("pipe", ("ctx", "dp"), None),
        P("pipe", None, ("ctx", "dp")),
    )
    return jax.shard_map(
        per_device, mesh=mesh, in_specs=in_specs, out_specs=out_specs, check_vma=False
    )
```

```python
import functools
import math

import jax
import jax.numpy as jnp
from jax import lax
from jax.experimental import pallas as pl
from jax.experimental.pallas import tpu as pltpu
from jax.sharding import PartitionSpec as P


HD = 128
KVH = 2
BLOCK = 64

epsilon = 1e-06


def chunk_sizes(blocks):
    sizes = [1] * min(2, blocks)
    while sum(sizes) < blocks:
        sizes.append(min(2, blocks - sum(sizes)))
    return sizes


def passed_along(block, axis, distance):
    devices = range(lax.axis_size(axis))
    route = [((i - distance) % len(devices), i) for i in devices]
    return lax.ppermute(block, axis, route)


def front_kernel(
    ranks, levels, hidden_hbm, gain_ref, gate_hbm, weight_ref, saved_hbm, kv_cot_hbm, gate_cot_hbm,
    normed_hbm, gating_ref, kv_hbm, grads_hbm,
    gate_ref, kv_cot_ref, gate_cot_ref, hidden_ref, normed_ref, saved_ref, full_ref, total_ref, kv_ref, grads_ref,
    load_sem, store_sem, send_sem, recv_sem, kv_send_sem, kv_recv_sem,
):
    pipe = lax.axis_index("pipe")
    mine = lax.axis_index("ctx")
    level = lax.axis_index("dp")
    across = lax.rem(mine + ranks // 2, ranks)
    beside = mine + 1 - 2 * lax.rem(mine, 2)
    corner = lax.rem(beside + ranks // 2, ranks)
    rows = weight_ref.shape[0]
    depth = levels * rows
    length, width = hidden_ref.shape
    tiles = kv_ref.shape[1]
    tile = length // tiles
    heads = gate_ref.shape[0]

    def at(rank, other):
        return (pipe, rank, other)

    loads = [
        pltpu.make_async_copy(hidden_hbm, hidden_ref, load_sem.at[0]),
        pltpu.make_async_copy(saved_hbm, saved_ref, load_sem.at[1]),
        pltpu.make_async_copy(weight_ref, full_ref.at[mine, level], load_sem.at[2]),
        pltpu.make_async_copy(kv_cot_hbm, kv_cot_ref, load_sem.at[3]),
        pltpu.make_async_copy(gate_cot_hbm, gate_cot_ref, load_sem.at[4]),
        pltpu.make_async_copy(gate_hbm, gate_ref, load_sem.at[5]),
    ]
    for load in loads:
        load.start()

    partners = [at(mine, lax.rem(level + d, levels)) for d in range(1, levels)]
    partners += [at(across, level), at(beside, level)]
    barrier = pltpu.get_barrier_semaphore()
    for partner in partners:
        pl.semaphore_signal(
            barrier, inc=1, device_id=partner, device_id_type=pl.DeviceIdType.MESH
        )
    pl.semaphore_wait(barrier, len(partners))

    sent = []

    def send(source, rank, other, target):
        copy = pltpu.make_async_remote_copy(
            src_ref=source,
            dst_ref=full_ref.at[rank, other],
            send_sem=send_sem.at[len(sent)],
            recv_sem=recv_sem.at[rank, other],
            device_id=target,
            device_id_type=pl.DeviceIdType.MESH,
        )
        copy.start()
        sent.append(copy)

    def arrived(rank, other):
        pltpu.make_async_remote_copy(
            src_ref=full_ref.at[rank, other],
            dst_ref=full_ref.at[rank, other],
            send_sem=send_sem.at[0],
            recv_sem=recv_sem.at[rank, other],
            device_id=at(beside, level),
            device_id_type=pl.DeviceIdType.MESH,
        ).wait_recv()

    send(weight_ref, mine, level, at(across, level))
    for d in range(1, levels):
        send(weight_ref, mine, level, at(mine, lax.rem(level + d, levels)))
    send(weight_ref, mine, level, at(beside, level))

    loads[0].wait()

    def norm_tile(i, carry):
        span = pl.ds(pl.multiple_of(i * 64, 64), 64)
        hidden = hidden_ref[span, :].astype(jnp.float32)
        scale = lax.rsqrt(jnp.mean(hidden * hidden, axis=-1, keepdims=True) + epsilon)
        normed_ref[span, :] = (hidden * scale * gain_ref[...]).astype(jnp.bfloat16)
        return carry

    lax.fori_loop(0, length // 64, norm_tile, 0)
    stores = []

    def store(source, target):
        copy = pltpu.make_async_copy(source, target, store_sem.at[len(stores)])
        copy.start()
        stores.append(copy)

    parts = grads_ref.shape[0]
    per_part = grads_ref.shape[1]
    columns = width // parts

    def grad_part(i):
        saved = saved_ref[:, i * columns : (i + 1) * columns]
        kv = lax.dot_general(
            saved, kv_cot_ref[...], (((0,), (0,)), ((), ())), preferred_element_type=jnp.float32
        )
        gate = lax.dot_general(
            gate_cot_ref[...], saved, (((0,), (0,)), ((), ())), preferred_element_type=jnp.float32
        )
        low = grads_ref.dtype
        grads_ref[i, :, :rows, :] = kv.reshape(per_part, rows, kv.shape[-1]).astype(low)
        grads_ref[i, :, rows:, :] = jnp.zeros_like(grads_ref[i, :, rows:, :])
        for k in range(per_part):
            grads_ref[i, k, rows : rows + heads, :rows] = gate[
                :, k * rows : (k + 1) * rows
            ].astype(low)

    for load in loads[1:]:
        load.wait()
    for d in range(max(levels, parts)):
        if d < levels - 1:
            other = lax.rem(level + levels - 1 - d, levels)
            arrived(mine, other)
            send(full_ref.at[mine, other], mine, other, at(across, level))
            send(full_ref.at[mine, other], mine, other, at(beside, level))
        if d < levels:
            other = lax.rem(level + levels - d, levels)
            arrived(across, other)
            send(full_ref.at[across, other], across, other, at(beside, level))
        if d < parts:
            grad_part(d)
            if d > 0:
                store(grads_ref.at[d - 1], grads_hbm.at[d - 1])
    store(normed_ref, normed_hbm)

    def term(rank, first, count):
        span = pl.ds(pl.multiple_of(rank * depth, 128), depth)
        return jnp.dot(
            normed_ref[first : first + count, span],
            full_ref[rank].reshape(depth, full_ref.shape[-1]),
            preferred_element_type=jnp.float32,
        )

    total_ref[...] = term(mine, 0, length)
    store(grads_ref.at[parts - 1], grads_hbm.at[parts - 1])
    total_ref[...] += term(across, 0, length)
    for d in range(levels):
        arrived(beside, lax.rem(level + levels - d, levels))
    total_ref[...] += term(beside, 0, length)
    for d in range(levels):
        arrived(corner, lax.rem(level + levels - d, levels))

    kv_sent = []

    def kv_send(rank, t, target):
        copy = pltpu.make_async_remote_copy(
            src_ref=kv_ref.at[rank, t],
            dst_ref=kv_ref.at[rank, t],
            send_sem=kv_send_sem.at[len(kv_sent)],
            recv_sem=kv_recv_sem.at[rank, t],
            device_id=target,
            device_id_type=pl.DeviceIdType.MESH,
        )
        copy.start()
        kv_sent.append(copy)

    def kv_arrived(rank, t):
        pltpu.make_async_remote_copy(
            src_ref=kv_ref.at[rank, t],
            dst_ref=kv_ref.at[rank, t],
            send_sem=kv_send_sem.at[0],
            recv_sem=kv_recv_sem.at[rank, t],
            device_id=at(beside, level),
            device_id_type=pl.DeviceIdType.MESH,
        ).wait_recv()

    def publish(t):
        kv_send(mine, t, at(across, level))
        kv_send(mine, t, at(beside, level))

    for t in range(tiles):
        span = slice(t * tile, (t + 1) * tile)
        projected = total_ref[span, :] + term(corner, t * tile, tile)
        kv_ref[mine, t] = projected.astype(jnp.bfloat16)
        if t > 0:
            publish(t - 1)
    logits = lax.dot_general(
        normed_ref[...], gate_ref[...], (((1,), (1,)), ((), ())),
        preferred_element_type=jnp.float32,
    )
    publish(tiles - 1)
    gating_ref[...] = jax.nn.sigmoid(logits)
    for t in range(tiles):
        kv_arrived(across, t)
        kv_send(across, t, at(beside, level))
    for t in range(tiles):
        kv_arrived(beside, t)
        kv_arrived(corner, t)
    store(kv_ref, kv_hbm)
    for copy in sent + kv_sent:
        copy.wait_send()
    for copy in stores:
        copy.wait()


def front(hidden, gain, gate_rows, weight, saved, kv_cot, gate_cot):
    ranks = lax.axis_size("ctx")
    levels = lax.axis_size("dp")
    length, width = hidden.shape
    heads = gate_rows.shape[0]
    rows, kv_width = weight.shape
    shards = ranks * levels
    parts = ranks
    tiles = 4
    padded = -(-heads // 16) * 16
    low, full = jnp.bfloat16, jnp.float32
    grads_shape = (parts, shards // parts, rows + padded, kv_width)
    kv_shape = (ranks, tiles, length // tiles, kv_width)
    vmem = pl.BlockSpec(memory_space=pltpu.VMEM)
    hbm = pl.BlockSpec(memory_space=pl.ANY)
    normed, gating, kv, grads = pl.pallas_call(
        functools.partial(front_kernel, ranks, levels),
        in_specs=[hbm, vmem, hbm, hbm, hbm, hbm, hbm],
        out_specs=[hbm, vmem, hbm, hbm],
        out_shape=[
            jax.ShapeDtypeStruct((length, width), low),
            jax.ShapeDtypeStruct((length, heads), full),
            jax.ShapeDtypeStruct(kv_shape, low),
            jax.ShapeDtypeStruct(grads_shape, low),
        ],
        scratch_shapes=[
            pltpu.VMEM(gate_rows.shape, low),
            pltpu.VMEM(kv_cot.shape, low),
            pltpu.VMEM(gate_cot.shape, low),
            pltpu.VMEM((length, width), low),
            pltpu.VMEM((length, width), low),
            pltpu.VMEM((length, width), low),
            pltpu.VMEM((ranks, levels, rows, kv_width), low),
            pltpu.VMEM((length, kv_width), full),
            pltpu.VMEM(kv_shape, low),
            pltpu.VMEM(grads_shape, low),
            pltpu.SemaphoreType.DMA((6,)),
            pltpu.SemaphoreType.DMA((parts + 2,)),
            pltpu.SemaphoreType.DMA((4 * levels - 1,)),
            pltpu.SemaphoreType.DMA((ranks, levels)),
            pltpu.SemaphoreType.DMA((3 * tiles,)),
            pltpu.SemaphoreType.DMA((ranks, tiles)),
        ],
        compiler_params=pltpu.CompilerParams(
            collective_id=0, has_side_effects=True, vmem_limit_bytes=60 * 2**20
        ),
    )(hidden, gain, gate_rows, weight, saved, kv_cot, gate_cot)
    return (
        normed,
        gating,
        kv.reshape(ranks * length, kv_width),
        grads.reshape(shards, rows + padded, kv_width),
    )


def attend_kernel(
    first, entries, picks_ref, place_ref, normed_ref, hidden_ref, gating_ref, kv_ref, out_ref,
    picked_ref, values_ref,
):
    step = first + pl.program_id(0)
    place = place_ref[0] + step
    keys = entries * BLOCK
    heads = gating_ref.shape[-1]
    group = heads // KVH
    half = group // 2
    scale = math.log2(math.e) / math.sqrt(HD)
    for c in range(entries):
        chosen = jnp.maximum(picks_ref[step, c], 0)
        tile = kv_ref[pl.ds(pl.multiple_of(chosen * BLOCK, BLOCK), BLOCK), :]
        span = slice(c * BLOCK, (c + 1) * BLOCK)
        for g in range(KVH):
            picked_ref[g, span, :] = tile[:, g * HD : (g + 1) * HD]
            values_ref[g, span, :HD] = tile[:, (KVH + g) * HD : (KVH + g + 1) * HD]
            values_ref[g, span, HD:] = jnp.ones((BLOCK, HD), jnp.bfloat16)
    column = lax.broadcasted_iota(jnp.int32, (BLOCK, keys), 1)
    row = lax.broadcasted_iota(jnp.int32, (BLOCK, keys), 0)
    last = jnp.where(column < BLOCK, row, (place + 1) * BLOCK - 1)
    bias = jnp.where(column <= last, 0.0, -1e30).astype(jnp.float32)
    gating = gating_ref[...]
    for g in range(KVH):
        k_all = picked_ref[g]
        v_all = values_ref[g]
        for part in range(0, group, half):
            first_head = g * group + part
            query = jnp.concatenate(
                [
                    normed_ref[:, (first_head + j) * HD : (first_head + j + 1) * HD]
                    for j in range(half)
                ],
                axis=0,
            )
            scores = lax.dot_general(
                query, k_all, (((1,), (1,)), ((), ())), preferred_element_type=jnp.float32
            )
            scores = (scores.reshape(half, BLOCK, keys) * scale + bias[None]).reshape(
                half * BLOCK, keys
            )
            top = jnp.max(scores, axis=-1, keepdims=True)
            weights = jnp.exp2(scores - top).astype(jnp.bfloat16)
            blended = jnp.dot(weights, v_all, preferred_element_type=jnp.float32)
            attended = blended[:, :HD] / blended[:, HD:]
            for j in range(half):
                h = first_head + j
                span = slice(h * HD, (h + 1) * HD)
                base = hidden_ref[:, span].astype(jnp.float32)
                piece = attended[j * BLOCK : (j + 1) * BLOCK]
                out_ref[:, span] = (base + gating[:, h : h + 1] * piece).astype(jnp.bfloat16)


def attend(first, count, picks, place, normed, hidden, gating, sequence_kv):
    width = normed.shape[1]
    heads = gating.shape[1]
    total, kv_width = sequence_kv.shape
    entries = picks.shape[1]
    return pl.pallas_call(
        functools.partial(attend_kernel, first, entries),
        grid_spec=pltpu.PrefetchScalarGridSpec(
            num_scalar_prefetch=2,
            grid=(count,),
            in_specs=[
                pl.BlockSpec((BLOCK, width), lambda i, *_: (first + i, 0)),
                pl.BlockSpec((BLOCK, width), lambda i, *_: (first + i, 0)),
                pl.BlockSpec((BLOCK, heads), lambda i, *_: (first + i, 0)),
                pl.BlockSpec((total, kv_width), lambda i, *_: (0, 0)),
            ],
            out_specs=pl.BlockSpec((BLOCK, width), lambda i, *_: (i, 0)),
            scratch_shapes=[
                pltpu.VMEM((KVH, entries * BLOCK, HD), jnp.bfloat16),
                pltpu.VMEM((KVH, entries * BLOCK, 2 * HD), jnp.bfloat16),
            ],
        ),
        out_shape=jax.ShapeDtypeStruct((count * BLOCK, width), jnp.bfloat16),
        cost_estimate=pl.CostEstimate(
            flops=6 * count * BLOCK * width * entries * BLOCK,
            bytes_accessed=6 * count * BLOCK * width + 2 * total * kv_width,
            transcendentals=count * BLOCK * heads * entries * BLOCK,
        ),
    )(picks, place, normed, hidden, gating, sequence_kv)


def per_device(
    hidden_in, selected, norm_gain, kv_weight, gate_weight, saved_norm, kv_cot, gate_cot
):
    current = hidden_in[0, 0]
    picks = selected[0, 0]
    length = current.shape[0]
    normed, gating, sequence_kv, grads = front(
        current, norm_gain, gate_weight[0], kv_weight[0], saved_norm[0, 0], kv_cot[0, 0],
        gate_cot[0, 0],
    )
    summed = lax.psum_scatter(grads, ("ctx", "dp"), scatter_dimension=0, tiled=True)[0]
    blocks_here = length // BLOCK
    place = (lax.axis_index("ctx") * blocks_here).astype(jnp.int32)[None]
    pieces = []
    first = 0
    for count in chunk_sizes(blocks_here):
        piece = attend(first, count, picks, place, normed, current, gating, sequence_kv)
        pieces.append(passed_along(piece, "pipe", 1))
        first += count
    passed = jnp.concatenate(pieces, axis=0)[None, None]
    rows = kv_weight.shape[1]
    heads = gate_weight.shape[1]
    kv_grad = summed[None, :rows].astype(jnp.bfloat16)
    gate_grad = summed[None, rows : rows + heads, :rows].astype(jnp.bfloat16)
    return (passed, kv_grad, gate_grad)


def solution(mesh):
    in_specs = (
        P("pipe", "dp", "ctx", None),
        P("pipe", "dp", "ctx", None),
        P("pipe", None),
        P("pipe", ("ctx", "dp"), None),
        P("pipe", None, None),
        P("pipe", "dp", "ctx", None),
        P("pipe", "dp", "ctx", None),
        P("pipe", "dp", "ctx", None),
    )
    out_specs = (
        P("pipe", "dp", "ctx", None),
        P("pipe", ("ctx", "dp"), None),
        P("pipe", None, ("ctx", "dp")),
    )
    return jax.shard_map(
        per_device, mesh=mesh, in_specs=in_specs, out_specs=out_specs, check_vma=False
    )
```
